256 devices in a mesh: dp: 32 (over x, z), expert: 8 (over y, core).
Axes of the slice: x: 4, y: 4, z: 8, core: 2. Of those that a mesh axis runs over, the one named last changes fastest.
Arguments:
- saved_inputs: bfloat16 [32, 8, 1024, 4096], P('dp', 'expert'), may hold values from -6 to 6
- saved_grads: bfloat16 [32, 8, 1024, 1536], P('dp', 'expert'), may hold values from -6 to 6
- row_counts: int32 [32, 8], P('dp', 'expert'), may hold values from 1 to 1024, as said below
- row_seq: int32 [32, 8, 1024], P('dp', 'expert'), may hold values from 0 to 255
- proj_in: bfloat16 [4096, 32], replicated, may hold values from -0.09375 to 0.09375
- proj_out: bfloat16 [1536, 32], replicated, may hold values from -0.15625 to 0.15625
Outputs:
- logged: bfloat16 [8, 8192, 1024], P(None, ('dp', 'expert'))
- fisher: float32 [1024, 8, 1024], P('dp', 'expert')
The draws below stay inside these ranges and needn't reach their ends.
Inputs may be any that keep to these rules, and one draw needn't show every extreme that they name: Slots from row_counts on are padding with arbitrary contents; row_counts reaches 1024 for some expert in every draw.
All inputs are finite; a program needn't handle non-finite values.
Results may differ from the reference program's by a relative error of at most 0.012.
Values may be sent and summed in bfloat16 or wider, within the bound.
No kernel may reach another device: no remote copies, remote signals or barrier semaphores. Data moves between devices by JAX's collectives and lax.ppermute only.
A program may use at most 64 MiB of HBM per device.

```python
import jax
import jax.numpy as jnp
from jax import lax

D = 4096
FF = 1536
K = 32
CAP = 1024
SEQ_DEV = 256
EXPERTS = 8
N_DP = 32


def draw_row_counts(key, part):
    key_fill = jax.random.fold_in(key, 11)
    key_star = jax.random.fold_in(key, 23)
    shard_ids = jnp.arange(N_DP, dtype=jnp.int32)[:, None]
    top_count = CAP - 2 * CAP // 3 * (N_DP - 1 - shard_ids) // max(N_DP - 1, 1)
    low_count = jnp.maximum(top_count // 4, 1)
    raw_bits = jax.random.randint(key_fill, (N_DP, EXPERTS), 0, 1 << 20)
    counts = low_count + raw_bits % (top_count - low_count + 1)
    star_expert = jax.random.randint(key_star, (), 0, EXPERTS)
    expert_ids = jnp.arange(EXPERTS, dtype=jnp.int32)[None, :]
    hit = (expert_ids == star_expert) & (shard_ids == N_DP - 1)
    return jnp.where(hit, CAP, counts).astype(jnp.int32)


def plant(result, own_key, low, largest):
    longest = result.shape.index(max(result.shape))
    spots = []
    for shift in (0, 1):
        where = [jax.random.randint(jax.random.fold_in(own_key, axis), (), 0, length) for axis, length in enumerate(result.shape)]
        where[longest] = (where[longest] + shift) % result.shape[longest]
        spots.append(tuple(where))
    return result.at[spots[0]].set(low).at[spots[1]].set(largest)


def steps_of(own_key, dims, cuts, smallest, largest):
    def one(axis_at, shards_of):
        draws = jax.random.uniform(jax.random.fold_in(jax.random.fold_in(own_key, 6), axis_at), (shards_of,), jnp.float32, smallest / len(cuts), largest / len(cuts))
        return jnp.repeat(jnp.exp(draws), dims[axis_at] // shards_of).reshape((-1,) + (1,) * (len(dims) - axis_at - 1))

    level = one(*cuts[0])
    for cut in cuts[1:]:
        level = level * one(*cut)
    return level


def bell_draw(key, extent, scale, limit, shards=(), kind=jnp.bfloat16):
    drawn = scale * jax.random.normal(key, extent, jnp.float32)
    if shards:
        drawn = drawn * steps_of(key, extent, shards, -0.22, 0.18)
    return jnp.clip(drawn, -limit, limit).astype(kind)


def setup_inputs(seed: int = 0) -> dict:
    seeds = jax.random.split(jax.random.key(seed), 7)
    return {
        "saved_inputs": bell_draw(seeds[0], (N_DP, EXPERTS, CAP, D), 1.0, 6.0, ((0, 32), (1, 8))),
        "saved_grads": bell_draw(seeds[1], (N_DP, EXPERTS, CAP, FF), 1.0, 6.0, ((0, 32), (1, 8))),
        "row_counts": draw_row_counts(jax.random.fold_in(seeds[6], 71), 0),
        "row_seq": plant(jax.random.randint(seeds[3], (N_DP, EXPERTS, CAP), 0, SEQ_DEV), jax.random.fold_in(seeds[3], 1), 0, SEQ_DEV - 1).astype(jnp.int32),
        "proj_in": bell_draw(seeds[4], (D, K), D ** -0.5, 0.09375),
        "proj_out": bell_draw(seeds[5], (FF, K), FF ** -0.5, 0.15625),
    }


def shard_grads(shard_data, proj_in, proj_out):
    inputs, row_grads, counts, seq_ids = shard_data
    experts, capacity, width = inputs.shape
    in_proj = jnp.dot(inputs.reshape(experts * capacity, width), proj_in, preferred_element_type=jnp.float32)
    out_proj = jnp.dot(row_grads.reshape(experts * capacity, row_grads.shape[2]), proj_out, preferred_element_type=jnp.float32)
    proj_rank = in_proj.shape[1]
    outer_rows = (out_proj[:, :, None] * in_proj[:, None, :]).reshape(experts, capacity, proj_rank * proj_rank).astype(jnp.bfloat16)
    slot_ids = jnp.arange(capacity, dtype=jnp.int32)
    is_live = slot_ids[None, :] < counts[:, None]
    member = (seq_ids[:, None, :] == jnp.arange(SEQ_DEV, dtype=jnp.int32)[None, :, None]) & is_live[:, None, :]
    onehot = member.astype(jnp.bfloat16)
    summed = jnp.einsum("esc,eck->esk", onehot.astype(jnp.float32), outer_rows.astype(jnp.float32))
    return summed.astype(jnp.bfloat16)


def reference(saved_inputs, saved_grads, row_counts, row_seq, proj_in, proj_out):
    per_shard = lax.map(lambda shard_data: shard_grads(shard_data, proj_in, proj_out),
                        (saved_inputs, saved_grads, row_counts, row_seq))
    logged = jnp.transpose(per_shard, (1, 0, 2, 3)).reshape(EXPERTS, N_DP * SEQ_DEV, K * K)
    widened = logged.astype(jnp.float32)
    fisher = jnp.einsum("esi,esj->iej", widened, widened, precision=lax.Precision.HIGHEST)
    totals = jnp.sum(row_counts.astype(jnp.float32), axis=0)
    return logged, fisher / totals[None, :, None]
```

```python
import functools

import jax
import jax.numpy as jnp
from jax import lax
from jax.experimental import pallas as pl
from jax.experimental.pallas import tpu as pltpu
from jax.sharding import Mesh
from jax.sharding import PartitionSpec as P

SEQ_DEV = 256
NX = 4
NZ = 8
K = 32
SQ = K * K
PANEL = SQ // NX
PIECE = PANEL // NZ
CAP = 1024
FAC = 72
ROWS = 256
VMEM_SPEC = pl.BlockSpec(memory_space=pltpu.VMEM)
SMEM_SPEC = pl.BlockSpec(memory_space=pltpu.SMEM)
NT = (((1,), (1,)), ((), ()))
TN = (((0,), (0,)), ((), ()))


def dot(a, b, dims):
    return lax.dot_general(a, b, dims, preferred_element_type=jnp.float32)


def project(cnt_ref, x_ref, g_ref, win_ref, wout_ref, seq_ref, fac_ref):
    i = pl.program_id(0)
    count = cnt_ref[0, 0]
    fac_ref[0:K, :] = dot(wout_ref[...], g_ref[...], NT).astype(jnp.bfloat16)
    fac_ref[K : 2 * K, :] = dot(win_ref[...], x_ref[...], NT).astype(jnp.bfloat16)
    slot = i * ROWS + lax.broadcasted_iota(jnp.int32, (8, ROWS), 1)
    row = lax.broadcasted_iota(jnp.int32, (8, ROWS), 0)
    seq = jnp.where(slot < count, jnp.broadcast_to(seq_ref[...], (8, ROWS)), SEQ_DEV)
    extra = jnp.where(row == 0, seq, jnp.where(row == 1, count >> 5, jnp.where(row == 2, count & 31, 0)))
    fac_ref[2 * K : FAC, :] = extra.astype(jnp.float32).astype(jnp.bfloat16)


def seq_grads(fac_ref, l_ref):
    seq = fac_ref[2 * K : FAC, :].astype(jnp.float32)[0:1, :]
    ids = lax.broadcasted_iota(jnp.int32, (SEQ_DEV, CAP), 0).astype(jnp.float32)
    onehot = jnp.where(ids == seq, 1.0, 0.0).astype(jnp.bfloat16)
    outs = fac_ref[0:K, :].astype(jnp.float32)
    ins = fac_ref[K : 2 * K, :].astype(jnp.float32)
    for c in range(NX):
        outer = jnp.concatenate(
            [(outs[k : k + 1, :] * ins).astype(jnp.bfloat16) for k in range(8 * c, 8 * c + 8)], axis=0
        )
        l_ref[:, c * PANEL : (c + 1) * PANEL] = dot(onehot, outer, NT).astype(jnp.bfloat16)


def panel_of(l_ref, x):
    mine = l_ref[:, pl.ds(pl.multiple_of(x * PANEL, PANEL), PANEL)]
    return dot(mine, l_ref[...], TN)


def own_part(x_ref, fac_ref, l_ref, p_ref):
    seq_grads(fac_ref, l_ref)
    p_ref[...] = panel_of(l_ref, x_ref[0])


def mid_part(x_ref, fa_ref, fb_ref, p0_ref, p_ref, l_ref):
    seq_grads(fa_ref, l_ref)
    acc = p0_ref[...] + panel_of(l_ref, x_ref[0])
    seq_grads(fb_ref, l_ref)
    p_ref[...] = acc + panel_of(l_ref, x_ref[0])


def last_part(x_ref, f0_ref, fa_ref, fb_ref, fc_ref, p1_ref, o_ref, l_ref):
    seq_grads(fc_ref, l_ref)
    total = p1_ref[...] + panel_of(l_ref, x_ref[0])
    for z in range(NZ):
        o_ref[z, :, 0:SQ] = total[z * PIECE : (z + 1) * PIECE, :].astype(jnp.bfloat16)
    extra = jnp.zeros((8, 128), jnp.float32)
    for ref in (f0_ref, fa_ref, fb_ref, fc_ref):
        extra = extra + ref[2 * K : FAC, 0:128].astype(jnp.float32)
    live = extra[1:2, :] * 32.0 + extra[2:3, :]
    high = jnp.floor(live * (1.0 / 64.0))
    low = live - high * 64.0
    row = lax.broadcasted_iota(jnp.int32, (PIECE, 128), 0)
    both = jnp.where(row == 0, high, jnp.where(row == 1, low, 0.0)).astype(jnp.bfloat16)
    for z in range(NZ):
        o_ref[z, :, SQ : SQ + 128] = both


def finish(r_ref, o_ref):
    total = jnp.zeros((PIECE, SQ + 128), jnp.float32)
    for z in range(NZ):
        total = total + r_ref[z].astype(jnp.float32)
    live = total[0:1, SQ : SQ + 1] * 64.0 + total[1:2, SQ : SQ + 1]
    o_ref[:, 0, :] = total[:, 0:SQ] / live


def shift(value, d):
    return lax.ppermute(value, "x", [(i, (i + d) % NX) for i in range(NX)])


def body(saved_inputs, saved_grads, row_counts, row_seq, proj_in, proj_out):
    width, ff = saved_inputs.shape[-1], saved_grads.shape[-1]
    x = lax.axis_index("x").astype(jnp.int32).reshape(1)
    fac = pl.pallas_call(
        project,
        grid=(CAP // ROWS,),
        in_specs=[
            SMEM_SPEC,
            pl.BlockSpec((ROWS, width), lambda i: (i, 0)),
            pl.BlockSpec((ROWS, ff), lambda i: (i, 0)),
            pl.BlockSpec((K, width), lambda i: (0, 0)),
            pl.BlockSpec((K, ff), lambda i: (0, 0)),
            pl.BlockSpec((1, ROWS), lambda i: (0, i)),
        ],
        out_specs=pl.BlockSpec((FAC, ROWS), lambda i: (0, i)),
        out_shape=jax.ShapeDtypeStruct((FAC, CAP), jnp.bfloat16),
        name="project",
    )(
        row_counts,
        saved_inputs.reshape(CAP, width),
        saved_grads.reshape(CAP, ff),
        proj_in.T,
        proj_out.T,
        row_seq.reshape(1, CAP),
    )
    far = shift(fac, 2)
    right = shift(fac, 1)
    left = shift(fac, 3)
    grads, part = pl.pallas_call(
        own_part,
        in_specs=[SMEM_SPEC, VMEM_SPEC],
        out_specs=[VMEM_SPEC, VMEM_SPEC],
        out_shape=[
            jax.ShapeDtypeStruct((SEQ_DEV, SQ), jnp.bfloat16),
            jax.ShapeDtypeStruct((PANEL, SQ), jnp.float32),
        ],
        name="own_part",
    )(x, fac)
    experts = lax.axis_size("expert")
    logged = lax.all_to_all(grads.reshape(experts, SEQ_DEV // experts, SQ), "expert", 0, 0, tiled=False)
    part = pl.pallas_call(
        mid_part,
        in_specs=[SMEM_SPEC] + [VMEM_SPEC] * 3,
        out_specs=VMEM_SPEC,
        out_shape=jax.ShapeDtypeStruct((PANEL, SQ), jnp.float32),
        scratch_shapes=[pltpu.VMEM((SEQ_DEV, SQ), jnp.bfloat16)],
        name="mid_part",
    )(x, right, left, part)
    pieces = pl.pallas_call(
        last_part,
        in_specs=[SMEM_SPEC] + [VMEM_SPEC] * 5,
        out_specs=VMEM_SPEC,
        out_shape=jax.ShapeDtypeStruct((NZ, PIECE, SQ + 128), jnp.bfloat16),
        scratch_shapes=[pltpu.VMEM((SEQ_DEV, SQ), jnp.bfloat16)],
        name="last_part",
    )(x, fac, right, left, far, part)
    got = lax.all_to_all(pieces, "z", 0, 0, tiled=False)
    fisher = pl.pallas_call(
        finish,
        in_specs=[VMEM_SPEC],
        out_specs=VMEM_SPEC,
        out_shape=jax.ShapeDtypeStruct((PIECE, 1, SQ), jnp.float32),
        name="finish",
    )(got)
    return (logged, fisher)


def solution(mesh):
    split = Mesh(mesh.devices.reshape(NX, NZ, mesh.shape["expert"]), ("x", "z", "expert"))
    dp = ("x", "z")
    in_specs = (
        P(dp, "expert", None, None),
        P(dp, "expert", None, None),
        P(dp, "expert"),
        P(dp, "expert", None),
        P(),
        P(),
    )
    out_specs = (P(None, ("x", "z", "expert"), None), P(dp, "expert", None))
    return jax.shard_map(body, mesh=split, in_specs=in_specs, out_specs=out_specs, check_vma=False)
```

```python
import jax
import jax.numpy as jnp
from jax import lax
from jax.experimental import pallas as pl
from jax.experimental.pallas import tpu as pltpu
from jax.sharding import Mesh
from jax.sharding import PartitionSpec as P


SEQ_DEV = 256
NX = 4
NZ = 8
K = 32
SQ = K * K
PANEL = SQ // NX
PIECE = PANEL // NZ
CAP = 1024
FAC = 72
CHUNKS = (
    (0, 0, 768),
    (0, 768, 768),
    (1, 0, 1024),
    (1, 1024, 1024),
    (1, 2048, 1024),
    (1, 3072, 512),
    (1, 3584, 512),
)
NSMALL = 2
MIB = 1 << 20
HBM_SPEC = pl.BlockSpec(memory_space=pltpu.MemorySpace.HBM)
SENT = (1, 6, 2, 5)
KEPT = (0, 7, 3, 4)
VMEM_SPEC = pl.BlockSpec(memory_space=pltpu.VMEM)
NT = (((1,), (1,)), ((), ()))
TN = (((0,), (0,)), ((), ()))


def dot(a, b, dims):
    return lax.dot_general(a, b, dims, preferred_element_type=jnp.float32)


def project(cnt_hbm, x_hbm, g_hbm, win_hbm, wout_hbm, seq_hbm, fac_ref, *scratch):
    cnt, win, wout, seq_row, sem, small = scratch[:6]
    parts = scratch[6:]
    first = [
        pltpu.make_async_copy(wout_hbm, wout, small.at[0]),
        pltpu.make_async_copy(win_hbm, win, small.at[1]),
        pltpu.make_async_copy(cnt_hbm, cnt, small.at[2]),
        pltpu.make_async_copy(seq_hbm, seq_row, small.at[3]),
    ]
    copies = []
    for i, (side, start, size) in enumerate(CHUNKS):
        source = (g_hbm, x_hbm)[side]
        copies.append(pltpu.make_async_copy(source.at[:, start : start + size], parts[i], sem.at[i]))
    first[0].start()
    copies[0].start()
    first[1].start()
    copies[1].start()
    first[2].start()
    first[3].start()
    for copy in copies[2:]:
        copy.start()
    sums = [None, None]
    first[0].wait()
    first[1].wait()
    for i, (side, start, size) in enumerate(CHUNKS):
        copies[i].wait()
        term = dot((wout, win)[side][:, start : start + size], parts[i][...], NT)
        sums[side] = term if sums[side] is None else sums[side] + term
        if i == NSMALL:
            first[2].wait()
            first[3].wait()
            count = cnt[0, 0]
            slot = lax.broadcasted_iota(jnp.int32, (8, CAP), 1)
            row = lax.broadcasted_iota(jnp.int32, (8, CAP), 0)
            seq = jnp.where(slot < count, jnp.broadcast_to(seq_row[...], (8, CAP)), SEQ_DEV)
            extra = jnp.where(row == 0, seq, jnp.where(row == 1, count >> 5, jnp.where(row == 2, count & 31, 0)))
            fac_ref[2 * K : FAC, :] = extra.astype(jnp.float32).astype(jnp.bfloat16)
            fac_ref[0:K, :] = sums[0].astype(jnp.bfloat16)
    fac_ref[K : 2 * K, :] = sums[1].astype(jnp.bfloat16)


def seq_grads(fac_ref, l_ref):
    seq = fac_ref[2 * K : FAC, :].astype(jnp.float32)[0:1, :]
    ids = lax.broadcasted_iota(jnp.int32, (SEQ_DEV, CAP), 0).astype(jnp.float32)
    onehot = jnp.where(ids == seq, 1.0, 0.0).astype(jnp.bfloat16)
    outs = fac_ref[0:K, :].astype(jnp.float32)
    ins = fac_ref[K : 2 * K, :].astype(jnp.float32)
    for c in range(NX):
        outer = jnp.concatenate(
            [(outs[k : k + 1, :] * ins).astype(jnp.bfloat16) for k in range(8 * c, 8 * c + 8)], axis=0
        )
        l_ref[:, c * PANEL : (c + 1) * PANEL] = dot(onehot, outer, NT).astype(jnp.bfloat16)


def panel_of(l_ref, x):
    mine = l_ref[:, pl.ds(pl.multiple_of(x * PANEL, PANEL), PANEL)]
    return dot(mine, l_ref[...], TN)


def own_part(fac_ref, l_ref, p_ref):
    seq_grads(fac_ref, l_ref)
    p_ref[...] = panel_of(l_ref, lax.axis_index("x"))


def mid_part(fa_ref, fb_ref, p0_ref, p_ref, l_ref):
    x = lax.axis_index("x")
    seq_grads(fa_ref, l_ref)
    acc = p0_ref[...] + panel_of(l_ref, x)
    seq_grads(fb_ref, l_ref)
    p_ref[...] = acc + panel_of(l_ref, x)


def last_part(f0_ref, fa_ref, fb_ref, fc_ref, p1_ref, sent_ref, kept_ref, l_ref, t_ref):
    x, z = lax.axis_index("x"), lax.axis_index("z")
    seq_grads(fc_ref, l_ref)
    t_ref[...] = p1_ref[...] + panel_of(l_ref, x)
    extra = jnp.zeros((8, 128), jnp.float32)
    for ref in (f0_ref, fa_ref, fb_ref, fc_ref):
        extra = extra + ref[2 * K : FAC, 0:128].astype(jnp.float32)
    live = extra[1:2, 0:1] * 32.0 + extra[2:3, 0:1]
    high = jnp.floor(live * (1.0 / 64.0))
    low = live - high * 64.0
    row = lax.broadcasted_iota(jnp.int32, (8, SQ), 0)
    lane = lax.broadcasted_iota(jnp.int32, (8, SQ), 1)
    for piece in range(NZ):
        rows = slice(piece * PIECE + PIECE - 8, (piece + 1) * PIECE)
        here = lane == (x * NZ + piece) * PIECE
        t_ref[rows, :] = jnp.where(here & (row == 7), high, jnp.where(here & (row == 6), low, t_ref[rows, :]))
    for ref, offsets in ((sent_ref, SENT), (kept_ref, KEPT)):
        for j, offset in enumerate(offsets):
            to = jnp.bitwise_xor(z, offset)
            rows = t_ref[pl.ds(pl.multiple_of(to * PIECE, PIECE), PIECE), :]
            ref[j] = rows.astype(ref.dtype)


def combine(kept_ref, got_ref, sent_ref, keep_ref):
    half = keep_ref.shape[0]
    for j in range(half):
        keep_ref[j] = kept_ref[j] + got_ref[j].astype(jnp.float32)
        sent_ref[j] = (kept_ref[half + j] + got_ref[half + j].astype(jnp.float32)).astype(jnp.bfloat16)


def finish(kept_ref, got_ref, o_ref):
    total = kept_ref[0] + got_ref[0].astype(jnp.float32)
    first = (lax.axis_index("x") * NZ + lax.axis_index("z")) * PIECE
    lane = lax.broadcasted_iota(jnp.int32, (1, SQ), 1)

    def pick(i, j):
        return jnp.sum(jnp.where(lane == first + j, total[i : i + 1, :], 0.0), axis=1, keepdims=True)

    live = pick(PIECE - 1, 0) * 64.0 + pick(PIECE - 2, 0)
    row = lax.broadcasted_iota(jnp.int32, (PIECE, SQ), 0)
    here = lax.broadcasted_iota(jnp.int32, (PIECE, SQ), 1) == first
    total = jnp.where(here & (row == PIECE - 1), pick(0, PIECE - 1), total)
    total = jnp.where(here & (row == PIECE - 2), pick(0, PIECE - 2), total)
    o_ref[:, 0, :] = total / live


def emit(l_ref, o_ref):
    o_ref[...] = l_ref[...]


def call(kernel, out, scratch=(), flops=0, vmem=14, in_specs=None, nin=0):
    return pl.pallas_call(
        kernel,
        in_specs=in_specs or [VMEM_SPEC] * nin,
        out_specs=[VMEM_SPEC] * len(out),
        out_shape=[jax.ShapeDtypeStruct(*o) for o in out],
        scratch_shapes=scratch,
        compiler_params=pltpu.CompilerParams(vmem_limit_bytes=vmem * MIB),
        cost_estimate=pl.CostEstimate(flops=flops, transcendentals=0, bytes_accessed=1 << 20),
    )


def shift(value, d):
    return lax.ppermute(value, "x", [(i, (i + d) % NX) for i in range(NX)])


def swap(value, d):
    return lax.ppermute(value, "z", [(i, i ^ d) for i in range(NZ)])


def step(saved_inputs, saved_grads, row_counts, row_seq, proj_in, proj_out):
    width, ff = saved_inputs.shape[-1], saved_grads.shape[-1]
    bf16, f32 = jnp.bfloat16, jnp.float32
    (fac,) = call(
        project,
        [((FAC, CAP), bf16)],
        [
            pltpu.SMEM((1, 1), jnp.int32),
            pltpu.VMEM((K, width), bf16),
            pltpu.VMEM((K, ff), bf16),
            pltpu.VMEM((1, CAP), jnp.int32),
            pltpu.SemaphoreType.DMA((len(CHUNKS),)),
            pltpu.SemaphoreType.DMA((4,)),
        ]
        + [pltpu.VMEM((CAP, size), bf16) for _, _, size in CHUNKS],
        in_specs=[HBM_SPEC] * 6,
        vmem=63,
    )(
        row_counts,
        saved_inputs.reshape(CAP, width),
        saved_grads.reshape(CAP, ff),
        proj_in.T,
        proj_out.T,
        row_seq.reshape(1, CAP),
    )
    far = shift(fac, 2)
    right = shift(fac, 1)
    left = shift(fac, 3)
    lbuf = pltpu.VMEM((SEQ_DEV, SQ), bf16)
    grads, part = call(own_part, [((SEQ_DEV, SQ), bf16), ((PANEL, SQ), f32)], nin=1, flops=1 << 30)(fac)
    experts = lax.axis_size("expert")
    logged = lax.all_to_all(grads.reshape(experts, SEQ_DEV // experts, SQ), "expert", 0, 0, tiled=False)
    (part,) = call(mid_part, [((PANEL, SQ), f32)], [lbuf], nin=3, flops=2 << 30)(right, left, part)
    sent, kept = call(
        last_part,
        [((4, PIECE, SQ), bf16), ((4, PIECE, SQ), f32)],
        [lbuf, pltpu.VMEM((PANEL, SQ), f32)],
        nin=5,
        flops=1 << 30,
    )(fac, right, left, far, part)
    got = swap(sent, 1)
    sent, kept = call(combine, [((2, PIECE, SQ), bf16), ((2, PIECE, SQ), f32)], nin=2)(kept, got)
    got = swap(sent, 3)
    sent, kept = call(combine, [((1, PIECE, SQ), bf16), ((1, PIECE, SQ), f32)], nin=2)(kept, got)
    got = swap(sent, 7)
    (logged,) = call(emit, [(logged.shape, bf16)], nin=1)(logged)
    (fisher,) = call(finish, [((PIECE, 1, SQ), f32)], nin=2)(kept, got)
    return (logged, fisher)


def solution(mesh):
    split = Mesh(mesh.devices.reshape(NX, NZ, mesh.shape["expert"]), ("x", "z", "expert"))
    dp = ("x", "z")
    in_specs = (
        P(dp, "expert", None, None),
        P(dp, "expert", None, None),
        P(dp, "expert"),
        P(dp, "expert", None),
        P(),
        P(),
    )
    out_specs = (P(None, ("x", "z", "expert"), None), P(dp, "expert", None))
    return jax.shard_map(step, mesh=split, in_specs=in_specs, out_specs=out_specs, check_vma=False)
```

```python
import jax
import jax.numpy as jnp
from jax import lax
from jax.experimental import pallas as pl
from jax.experimental.pallas import tpu as pltpu
from jax.sharding import Mesh
from jax.sharding import PartitionSpec as P


SEQ_DEV = 256
NX = 4
NZ = 8
K = 32
SQ = K * K
PANEL = SQ // NX
PIECE = PANEL // NZ
CAP = 1024
FAC = 72
HALF_CAP = CAP // 2
MIB = 1 << 20
HBM_SPEC = pl.BlockSpec(memory_space=pltpu.MemorySpace.HBM)
ROUNDS = (1, 7, 3)
VMEM_SPEC = pl.BlockSpec(memory_space=pltpu.VMEM)
NT = (((1,), (1,)), ((), ()))
TN = (((0,), (0,)), ((), ()))


def dot(a, b, dims):
    return lax.dot_general(a, b, dims, preferred_element_type=jnp.float32)


def project(cnt_ref, x_hbm, g_hbm, win_hbm, wout_hbm, seq_hbm, fac_ref, win, wout, seq_row, x0, x1, g, sem):
    low, high = slice(0, HALF_CAP), slice(HALF_CAP, CAP)
    copy_win = pltpu.make_async_copy(win_hbm, win, sem.at[0])
    copy_wout = pltpu.make_async_copy(wout_hbm, wout, sem.at[1])
    copy_seq = pltpu.make_async_copy(seq_hbm, seq_row, sem.at[2])
    copy_x0 = pltpu.make_async_copy(x_hbm.at[low], x0, sem.at[3])
    copy_x1 = pltpu.make_async_copy(x_hbm.at[high], x1, sem.at[4])
    copy_g = pltpu.make_async_copy(g_hbm, g, sem.at[5])
    copy_win.start()
    copy_x0.start()
    copy_x1.start()
    copy_wout.start()
    copy_seq.start()
    copy_win.wait()
    copy_x0.wait()
    copy_g.start()
    fac_ref[K : 2 * K, low] = dot(win[...], x0[...], NT).astype(jnp.bfloat16)
    copy_seq.wait()
    count = jnp.broadcast_to(cnt_ref[...], (8, CAP))
    slot = lax.broadcasted_iota(jnp.int32, (8, CAP), 1)
    row = lax.broadcasted_iota(jnp.int32, (8, CAP), 0)
    seq = jnp.where(slot < count, jnp.broadcast_to(seq_row[...], (8, CAP)), SEQ_DEV)
    extra = jnp.where(row == 0, seq, jnp.where(row == 1, count >> 5, jnp.where(row == 2, count & 31, 0)))
    fac_ref[2 * K : FAC, :] = extra.astype(jnp.float32).astype(jnp.bfloat16)
    copy_x1.wait()
    fac_ref[K : 2 * K, high] = dot(win[...], x1[...], NT).astype(jnp.bfloat16)
    copy_wout.wait()
    copy_g.wait()
    fac_ref[0:K, :] = dot(wout[...], g[...], NT).astype(jnp.bfloat16)


def seq_grads(fac_ref, l_ref):
    seq = fac_ref[2 * K : FAC, :].astype(jnp.float32)[0:1, :]
    ids = lax.broadcasted_iota(jnp.int32, (SEQ_DEV, CAP), 0).astype(jnp.float32)
    onehot = jnp.where(ids == seq, 1.0, 0.0).astype(jnp.bfloat16)
    outs = fac_ref[0:K, :].astype(jnp.float32)
    ins = fac_ref[K : 2 * K, :].astype(jnp.float32)
    for c in range(NX):
        outer = jnp.concatenate(
            [(outs[k : k + 1, :] * ins).astype(jnp.bfloat16) for k in range(8 * c, 8 * c + 8)], axis=0
        )
        l_ref[:, c * PANEL : (c + 1) * PANEL] = dot(onehot, outer, NT).astype(jnp.bfloat16)


def panel_of(l_ref, x):
    mine = l_ref[:, pl.ds(pl.multiple_of(x * PANEL, PANEL), PANEL)]
    return dot(mine, l_ref[...], TN)


def own_part(fac_ref, l_ref, p_ref):
    seq_grads(fac_ref, l_ref)
    p_ref[...] = panel_of(l_ref, lax.axis_index("x"))


def mid_part(fa_ref, fb_ref, p0_ref, p_ref, l_ref):
    x = lax.axis_index("x")
    seq_grads(fa_ref, l_ref)
    acc = p0_ref[...] + panel_of(l_ref, x)
    seq_grads(fb_ref, l_ref)
    p_ref[...] = acc + panel_of(l_ref, x)


def hop(z, d):
    return lax.rem(z + jnp.where(lax.rem(z, 2) == 0, d, NZ - d), NZ)


def last_part(f0_ref, fa_ref, fb_ref, fc_ref, p1_ref, sent_ref, kept_ref, l_ref, t_ref):
    x, z = lax.axis_index("x"), lax.axis_index("z")
    seq_grads(fc_ref, l_ref)
    t_ref[...] = p1_ref[...] + panel_of(l_ref, x)
    extra = jnp.zeros((8, 128), jnp.float32)
    for ref in (f0_ref, fa_ref, fb_ref, fc_ref):
        extra = extra + ref[2 * K : FAC, 0:128].astype(jnp.float32)
    live = extra[1:2, 0:1] * 32.0 + extra[2:3, 0:1]
    high = jnp.floor(live * (1.0 / 64.0))
    low = live - high * 64.0
    row = lax.broadcasted_iota(jnp.int32, (8, SQ), 0)
    lane = lax.broadcasted_iota(jnp.int32, (8, SQ), 1)
    for piece in range(NZ):
        rows = slice(piece * PIECE + PIECE - 8, (piece + 1) * PIECE)
        here = lane == (x * NZ + piece) * PIECE
        t_ref[rows, :] = jnp.where(here & (row == 7), high, jnp.where(here & (row == 6), low, t_ref[rows, :]))
    first, second, third = ROUNDS
    to = hop(z, first)
    for ref, order in (
        (sent_ref, (to, hop(to, third), hop(to, second), hop(hop(to, second), third))),
        (kept_ref, (z, hop(z, third), hop(z, second), hop(hop(z, second), third))),
    ):
        for j, piece in enumerate(order):
            rows = t_ref[pl.ds(pl.multiple_of(piece * PIECE, PIECE), PIECE), :]
            ref[j] = rows.astype(ref.dtype)


def combine(kept_ref, got_ref, sent_ref, keep_ref):
    half = keep_ref.shape[0]
    for j in range(half):
        keep_ref[j] = kept_ref[j] + got_ref[j].astype(jnp.float32)
        sent_ref[j] = (kept_ref[half + j] + got_ref[half + j].astype(jnp.float32)).astype(jnp.bfloat16)


def finish(kept_ref, got_ref, o_ref):
    total = kept_ref[0] + got_ref[0].astype(jnp.float32)
    first = (lax.axis_index("x") * NZ + lax.axis_index("z")) * PIECE
    lane = lax.broadcasted_iota(jnp.int32, (1, SQ), 1)

    def pick(i, j):
        return jnp.sum(jnp.where(lane == first + j, total[i : i + 1, :], 0.0), axis=1, keepdims=True)

    live = pick(PIECE - 1, 0) * 64.0 + pick(PIECE - 2, 0)
    row = lax.broadcasted_iota(jnp.int32, (PIECE, SQ), 0)
    here = lax.broadcasted_iota(jnp.int32, (PIECE, SQ), 1) == first
    total = jnp.where(here & (row == PIECE - 1), pick(0, PIECE - 1), total)
    total = jnp.where(here & (row == PIECE - 2), pick(0, PIECE - 2), total)
    o_ref[:, 0, :] = total / live


def emit(l_ref, o_ref):
    o_ref[...] = l_ref[...]


def call(kernel, out, scratch=(), flops=0, vmem=14, in_specs=None, nin=0):
    return pl.pallas_call(
        kernel,
        in_specs=in_specs or [VMEM_SPEC] * nin,
        out_specs=[VMEM_SPEC] * len(out),
        out_shape=[jax.ShapeDtypeStruct(*o) for o in out],
        scratch_shapes=scratch,
        compiler_params=pltpu.CompilerParams(vmem_limit_bytes=vmem * MIB),
        cost_estimate=pl.CostEstimate(flops=flops, transcendentals=0, bytes_accessed=1 << 20),
    )


def shift(value, d):
    return lax.ppermute(value, "x", [(i, (i + d) % NX) for i in range(NX)])


def swap(value, d):
    pairs = [(i, (i + (d if i % 2 == 0 else NZ - d)) % NZ) for i in range(NZ)]
    return lax.ppermute(value, "z", pairs)


def step(saved_inputs, saved_grads, row_counts, row_seq, proj_in, proj_out):
    width, ff = saved_inputs.shape[-1], saved_grads.shape[-1]
    bf16, f32 = jnp.bfloat16, jnp.float32
    (fac,) = call(
        project,
        [((FAC, CAP), bf16)],
        [
            pltpu.VMEM((K, width), bf16),
            pltpu.VMEM((K, ff), bf16),
            pltpu.VMEM((1, CAP), jnp.int32),
            pltpu.VMEM((HALF_CAP, width), bf16),
            pltpu.VMEM((HALF_CAP, width), bf16),
            pltpu.VMEM((CAP, ff), bf16),
            pltpu.SemaphoreType.DMA((6,)),
        ],
        in_specs=[VMEM_SPEC] + [HBM_SPEC] * 5,
        vmem=24,
    )(
        row_counts,
        *(
            pltpu.with_memory_space_constraint(value, pltpu.MemorySpace.HBM)
            for value in (
                saved_inputs.reshape(CAP, width),
                saved_grads.reshape(CAP, ff),
                proj_in.T,
                proj_out.T,
                row_seq.reshape(1, CAP),
            )
        ),
    )
    far = shift(fac, 2)
    right = shift(fac, 1)
    left = shift(fac, 3)
    lbuf = pltpu.VMEM((SEQ_DEV, SQ), bf16)
    grads, part = call(own_part, [((SEQ_DEV, SQ), bf16), ((PANEL, SQ), f32)], nin=1, flops=1 << 30)(fac)
    experts = lax.axis_size("expert")
    logged = lax.all_to_all(grads.reshape(experts, SEQ_DEV // experts, SQ), "expert", 0, 0, tiled=False)
    (part,) = call(mid_part, [((PANEL, SQ), f32)], [lbuf], nin=3, flops=2 << 30)(right, left, part)
    sent, kept = call(
        last_part,
        [((4, PIECE, SQ), bf16), ((4, PIECE, SQ), f32)],
        [lbuf, pltpu.VMEM((PANEL, SQ), f32)],
        nin=5,
        flops=1 << 30,
    )(fac, right, left, far, part)
    got = swap(sent, 1)
    sent, kept = call(combine, [((2, PIECE, SQ), bf16), ((2, PIECE, SQ), f32)], nin=2)(kept, got)
    got = swap(sent, 7)
    sent, kept = call(combine, [((1, PIECE, SQ), bf16), ((1, PIECE, SQ), f32)], nin=2)(kept, got)
    got = swap(sent, 3)
    (logged,) = call(emit, [(logged.shape, bf16)], nin=1)(logged)
    (fisher,) = call(finish, [((PIECE, 1, SQ), f32)], nin=2)(kept, got)
    return (logged, fisher)


def solution(mesh):
    split = Mesh(mesh.devices.reshape(NX, NZ, mesh.shape["expert"]), ("x", "z", "expert"))
    dp = ("x", "z")
    in_specs = (
        P(dp, "expert", None, None),
        P(dp, "expert", None, None),
        P(dp, "expert"),
        P(dp, "expert", None),
        P(),
        P(),
    )
    out_specs = (P(None, ("x", "z", "expert"), None), P(dp, "expert", None))
    return jax.shard_map(step, mesh=split, in_specs=in_specs, out_specs=out_specs, check_vma=False)
```

```python
import jax
import jax.numpy as jnp
from jax import lax
from jax.experimental import pallas as pl
from jax.experimental.pallas import tpu as pltpu
from jax.sharding import Mesh
from jax.sharding import PartitionSpec as P


SEQ_DEV = 256
NX = 4
NZ = 8
K = 32
SQ = K * K
PANEL = SQ // NX
PIECE = PANEL // NZ
CAP = 1024
FAC = 72
HALF_CAP = CAP // 2
MIB = 1 << 20
HBM_SPEC = pl.BlockSpec(memory_space=pltpu.MemorySpace.HBM)
ROUNDS = (1, 7, 3)
VMEM_SPEC = pl.BlockSpec(memory_space=pltpu.VMEM)
NT = (((1,), (1,)), ((), ()))
TN = (((0,), (0,)), ((), ()))


def dot(a, b, dims):
    return lax.dot_general(a, b, dims, preferred_element_type=jnp.float32)


def project(cnt_ref, x_hbm, g_hbm, win_hbm, wout_hbm, seq_hbm, fac_ref, win, wout, seq_row, x0, x1, g, sem):
    low, high = slice(0, HALF_CAP), slice(HALF_CAP, CAP)
    copy_win = pltpu.make_async_copy(win_hbm, win, sem.at[0])
    copy_wout = pltpu.make_async_copy(wout_hbm, wout, sem.at[1])
    copy_seq = pltpu.make_async_copy(seq_hbm, seq_row, sem.at[2])
    copy_x0 = pltpu.make_async_copy(x_hbm.at[low], x0, sem.at[3])
    copy_x1 = pltpu.make_async_copy(x_hbm.at[high], x1, sem.at[4])
    copy_g = pltpu.make_async_copy(g_hbm, g, sem.at[5])
    copy_win.start()
    copy_x0.start()
    copy_x1.start()
    copy_wout.start()
    copy_seq.start()
    copy_win.wait()
    copy_x0.wait()
    copy_g.start()
    fac_ref[K : 2 * K, low] = dot(win[...], x0[...], NT).astype(jnp.bfloat16)
    copy_seq.wait()
    count = jnp.broadcast_to(cnt_ref[...], (8, CAP))
    slot = lax.broadcasted_iota(jnp.int32, (8, CAP), 1)
    row = lax.broadcasted_iota(jnp.int32, (8, CAP), 0)
    seq = jnp.where(slot < count, jnp.broadcast_to(seq_row[...], (8, CAP)), SEQ_DEV)
    extra = jnp.where(row == 0, seq, jnp.where(row == 1, count >> 5, jnp.where(row == 2, count & 31, 0)))
    fac_ref[2 * K : FAC, :] = extra.astype(jnp.float32).astype(jnp.bfloat16)
    copy_x1.wait()
    fac_ref[K : 2 * K, high] = dot(win[...], x1[...], NT).astype(jnp.bfloat16)
    copy_wout.wait()
    copy_g.wait()
    fac_ref[0:K, :] = dot(wout[...], g[...], NT).astype(jnp.bfloat16)


def seq_grads(fac_ref, l_ref):
    seq = fac_ref[2 * K : FAC, :].astype(jnp.float32)[0:1, :]
    ids = lax.broadcasted_iota(jnp.int32, (SEQ_DEV, CAP), 0).astype(jnp.float32)
    onehot = jnp.where(ids == seq, 1.0, 0.0).astype(jnp.bfloat16)
    outs = fac_ref[0:K, :].astype(jnp.float32)
    ins = fac_ref[K : 2 * K, :].astype(jnp.float32)
    for c in range(NX):
        outer = jnp.concatenate(
            [(outs[k : k + 1, :] * ins).astype(jnp.bfloat16) for k in range(8 * c, 8 * c + 8)], axis=0
        )
        l_ref[:, c * PANEL : (c + 1) * PANEL] = dot(onehot, outer, NT).astype(jnp.bfloat16)


def panel_of(l_ref, x):
    mine = l_ref[:, pl.ds(pl.multiple_of(x * PANEL, PANEL), PANEL)]
    return dot(mine, l_ref[...], TN)


def own_part(fac_ref, l_ref, p_ref):
    seq_grads(fac_ref, l_ref)
    p_ref[...] = panel_of(l_ref, lax.axis_index("x"))


def mid_part(fac_ref, p0_ref, p_ref, l_ref):
    seq_grads(fac_ref, l_ref)
    p_ref[...] = p0_ref[...] + panel_of(l_ref, lax.axis_index("x"))


def hop(z, d):
    return lax.rem(z + jnp.where(lax.rem(z, 2) == 0, d, NZ - d), NZ)


def last_part(f0_ref, fa_ref, fb_ref, fc_ref, p1_ref, sent_ref, kept_ref, l_ref, t_ref):
    x, z = lax.axis_index("x"), lax.axis_index("z")
    seq_grads(fc_ref, l_ref)
    t_ref[...] = p1_ref[...] + panel_of(l_ref, x)
    extra = jnp.zeros((8, 128), jnp.float32)
    for ref in (f0_ref, fa_ref, fb_ref, fc_ref):
        extra = extra + ref[2 * K : FAC, 0:128].astype(jnp.float32)
    live = extra[1:2, 0:1] * 32.0 + extra[2:3, 0:1]
    high = jnp.floor(live * (1.0 / 64.0))
    low = live - high * 64.0
    row = lax.broadcasted_iota(jnp.int32, (8, SQ), 0)
    lane = lax.broadcasted_iota(jnp.int32, (8, SQ), 1)
    for piece in range(NZ):
        rows = slice(piece * PIECE + PIECE - 8, (piece + 1) * PIECE)
        here = lane == (x * NZ + piece) * PIECE
        t_ref[rows, :] = jnp.where(here & (row == 7), high, jnp.where(here & (row == 6), low, t_ref[rows, :]))
    first, second, third = ROUNDS
    to = hop(z, first)
    for ref, order in (
        (sent_ref, (to, hop(to, third), hop(to, second), hop(hop(to, second), third))),
        (kept_ref, (z, hop(z, third), hop(z, second), hop(hop(z, second), third))),
    ):
        for j, piece in enumerate(order):
            rows = t_ref[pl.ds(pl.multiple_of(piece * PIECE, PIECE), PIECE), :]
            ref[j] = rows.astype(ref.dtype)


def combine(kept_ref, got_ref, sent_ref, keep_ref):
    half = keep_ref.shape[0]
    for j in range(half):
        keep_ref[j] = kept_ref[j] + got_ref[j].astype(jnp.float32)
        sent_ref[j] = (kept_ref[half + j] + got_ref[half + j].astype(jnp.float32)).astype(jnp.bfloat16)


def finish(kept_ref, got_ref, o_ref):
    total = kept_ref[0] + got_ref[0].astype(jnp.float32)
    first = (lax.axis_index("x") * NZ + lax.axis_index("z")) * PIECE
    lane = lax.broadcasted_iota(jnp.int32, (1, SQ), 1)

    def pick(i, j):
        return jnp.sum(jnp.where(lane == first + j, total[i : i + 1, :], 0.0), axis=1, keepdims=True)

    live = pick(PIECE - 1, 0) * 64.0 + pick(PIECE - 2, 0)
    row = lax.broadcasted_iota(jnp.int32, (PIECE, SQ), 0)
    here = lax.broadcasted_iota(jnp.int32, (PIECE, SQ), 1) == first
    total = jnp.where(here & (row == PIECE - 1), pick(0, PIECE - 1), total)
    total = jnp.where(here & (row == PIECE - 2), pick(0, PIECE - 2), total)
    o_ref[:, 0, :] = total / live


def emit(l_ref, o_ref):
    o_ref[...] = l_ref[...]


def call(kernel, out, scratch=(), flops=0, vmem=14, in_specs=None, nin=0):
    return pl.pallas_call(
        kernel,
        in_specs=in_specs or [VMEM_SPEC] * nin,
        out_specs=[VMEM_SPEC] * len(out),
        out_shape=[jax.ShapeDtypeStruct(*o) for o in out],
        scratch_shapes=scratch,
        compiler_params=pltpu.CompilerParams(vmem_limit_bytes=vmem * MIB),
        cost_estimate=pl.CostEstimate(flops=flops, transcendentals=0, bytes_accessed=1 << 20),
    )


def shift(value, d):
    return lax.ppermute(value, "x", [(i, (i + d) % NX) for i in range(NX)])


def swap(value, d):
    pairs = [(i, (i + (d if i % 2 == 0 else NZ - d)) % NZ) for i in range(NZ)]
    return lax.ppermute(value, "z", pairs)


def step(saved_inputs, saved_grads, row_counts, row_seq, proj_in, proj_out):
    width, ff = saved_inputs.shape[-1], saved_grads.shape[-1]
    bf16, f32 = jnp.bfloat16, jnp.float32
    (fac,) = call(
        project,
        [((FAC, CAP), bf16)],
        [
            pltpu.VMEM((K, width), bf16),
            pltpu.VMEM((K, ff), bf16),
            pltpu.VMEM((1, CAP), jnp.int32),
            pltpu.VMEM((HALF_CAP, width), bf16),
            pltpu.VMEM((HALF_CAP, width), bf16),
            pltpu.VMEM((CAP, ff), bf16),
            pltpu.SemaphoreType.DMA((6,)),
        ],
        in_specs=[VMEM_SPEC] + [HBM_SPEC] * 5,
        vmem=24,
    )(
        row_counts,
        *(
            pltpu.with_memory_space_constraint(value, pltpu.MemorySpace.HBM)
            for value in (
                saved_inputs.reshape(CAP, width),
                saved_grads.reshape(CAP, ff),
                proj_in.T,
                proj_out.T,
                row_seq.reshape(1, CAP),
            )
        ),
    )
    far = shift(fac, 2)
    right = shift(fac, 1)
    left = shift(fac, 3)
    lbuf = pltpu.VMEM((SEQ_DEV, SQ), bf16)
    grads, part = call(own_part, [((SEQ_DEV, SQ), bf16), ((PANEL, SQ), f32)], nin=1, flops=1 << 30)(fac)
    experts = lax.axis_size("expert")
    logged = lax.all_to_all(grads.reshape(experts, SEQ_DEV // experts, SQ), "expert", 0, 0, tiled=False)
    for other in (right, left):
        (part,) = call(mid_part, [((PANEL, SQ), f32)], [lbuf], nin=2, flops=1 << 30)(other, part)
    sent, kept = call(
        last_part,
        [((4, PIECE, SQ), bf16), ((4, PIECE, SQ), f32)],
        [lbuf, pltpu.VMEM((PANEL, SQ), f32)],
        nin=5,
        flops=1 << 30,
    )(fac, right, left, far, part)
    got = swap(sent, 1)
    sent, kept = call(combine, [((2, PIECE, SQ), bf16), ((2, PIECE, SQ), f32)], nin=2)(kept, got)
    got = swap(sent, 7)
    sent, kept = call(combine, [((1, PIECE, SQ), bf16), ((1, PIECE, SQ), f32)], nin=2)(kept, got)
    got = swap(sent, 3)
    (logged,) = call(emit, [(logged.shape, bf16)], nin=1)(logged)
    (fisher,) = call(finish, [((PIECE, 1, SQ), f32)], nin=2)(kept, got)
    return (logged, fisher)


def solution(mesh):
    split = Mesh(mesh.devices.reshape(NX, NZ, mesh.shape["expert"]), ("x", "z", "expert"))
    dp = ("x", "z")
    in_specs = (
        P(dp, "expert", None, None),
        P(dp, "expert", None, None),
        P(dp, "expert"),
        P(dp, "expert", None),
        P(),
        P(),
    )
    out_specs = (P(None, ("x", "z", "expert"), None), P(dp, "expert", None))
    return jax.shard_map(step, mesh=split, in_specs=in_specs, out_specs=out_specs, check_vma=False)
```
